512 devices in a mesh: dp: 64 (over z, x_lo, core), head: 8 (over x_hi, y).
Axes of the slice: x: 4 (x_hi: 2, x_lo: 2; x = x_hi * 2 + x_lo), y: 4, z: 16, core: 2. Of those that a mesh axis runs over, the one named last changes fastest.
Arguments:
- layer_input: bfloat16 [65536, 8192], P('dp', 'head'), may hold values from -0.09375 to 0.09375
- query_states: bfloat16 [65536, 4096], P(('dp', 'head')), may hold values from -7.5 to 7.5
- key_states: bfloat16 [65536, 1024], P(('dp', 'head')), may hold values from -6 to 6
- value_states: bfloat16 [65536, 1024], P(('dp', 'head')), may hold values from -6 to 6
- out_grad: bfloat16 [65536, 4096], P(('dp', 'head')), may hold values from -6 to 6
- parents: int32 [65536], P('dp'), may hold values from 0 to 510, as said below
- lengths: int32 [128], P('dp'), may hold values from 1 to 512, 40960 in all
Outputs:
- weight_gradient: float32 [1024, 8192], P('dp', 'head')
- value_gradient: bfloat16 [65536, 1024], P(('dp', 'head'))
The draws below stay inside these ranges and needn't reach their ends.
Inputs may be any that keep to these rules, and one draw needn't show every extreme that they name: `parents`: within each tree a token's parent is an earlier token of the same tree; the first token of a tree is its own parent. The lengths of all trees sum to 40960.
All inputs are finite; a program needn't handle non-finite values. No bound on the sum of `lengths` on one device may be relied on, other than what follows from the above.
Results may differ from the reference program's by a relative error of at most 0.0049.
Values may be sent and summed in bfloat16 or wider, within the bound.
No kernel may reach another device: no remote copies, remote signals or barrier semaphores. Data moves between devices by JAX's collectives and lax.ppermute only.
A program may use at most 64 MiB of HBM per device.

```python
import math
import jax
import jax.numpy as jnp
import numpy as np
from jax import lax

D = 8192
Q_HEADS = 32
KV_HEADS = 8
HEAD_DIM = 128
TREE_LEN = 512
TREES = 128
TOKENS = 65536


def paired_states(key):
    query_shape = (TOKENS, Q_HEADS * HEAD_DIM)
    key_shape = (TOKENS, KV_HEADS * HEAD_DIM)
    query_states = jnp.clip(jax.random.normal(jax.random.fold_in(key, 31), query_shape, jnp.float32), -6.0, 6.0)
    key_states = jnp.clip(jax.random.normal(jax.random.fold_in(key, 32), key_shape, jnp.float32), -6.0, 6.0)
    return (query_states, key_states)


def draw_query_states(key, part):
    return paired_states(key)[0].astype(jnp.bfloat16)


def draw_key_states(key, part):
    return paired_states(key)[1].astype(jnp.bfloat16)


def draw_parents(key, part):
    position = jnp.arange(TOKENS, dtype=jnp.int32) % TREE_LEN
    fork_draw = jax.random.randint(jax.random.fold_in(key, 41), (TOKENS,), 0, 16)
    forked = (fork_draw == 0) & (position > 0) & (position % 64 != 5) & (position != TREE_LEN - 1)
    earlier = jax.random.randint(jax.random.fold_in(key, 42), (TOKENS,), 0, jnp.maximum(position, 1))
    return jnp.where(forked, earlier, jnp.maximum(position - 1, 0)).astype(jnp.int32)


def block_scale(stream_key, extent, cuts, least, top_value):
    def one(axis_at, blocks):
        steps = jax.random.uniform(jax.random.fold_in(jax.random.fold_in(stream_key, 6), axis_at), (blocks,), jnp.float32, least / len(cuts), top_value / len(cuts))
        return jnp.repeat(jnp.exp(steps), extent[axis_at] // blocks).reshape((-1,) + (1,) * (len(extent) - axis_at - 1))

    gain = one(*cuts[0])
    for cut in cuts[1:]:
        gain = gain * one(*cut)
    return gain


def split_up(count, total, limit, lean):
    portions = [(1 << 20) // math.isqrt(grade ** lean) + 1 for grade in range(2, count + 1)]
    spare, counts = total - limit - (count - 1), [1] * (count - 1)
    while spare > 0:
        candidates = [i for i in range(count - 1) if counts[i] < limit]
        pool, left = sum([portions[i] for i in candidates]), spare
        for i in candidates:
            more = min(limit - counts[i], max(1, left * portions[i] // pool), spare)
            counts[i] = counts[i] + more
            spare = spare - more
    return np.array([limit] + counts)


def ragged_sizes(rng, amount, total, limit, slope):
    if amount == 2:
        one = jax.random.randint(rng, (), max(1, total - limit), min(limit, total - 1) + 1)
        return jnp.stack([one, total - one])
    sizes = jnp.asarray(split_up(amount, total, limit, slope), jnp.int32)
    twos = (amount - 1) // 2
    giver, sink = sizes[1:1 + 2 * twos:2], sizes[2:2 + 2 * twos:2]
    room = jnp.minimum(giver - 1, limit - sink)
    shifted = jax.random.randint(jax.random.fold_in(rng, 1), (twos,), 0, 1 << 20) % (room + 1)
    sizes = sizes.at[1:1 + 2 * twos:2].set(giver - shifted).at[2:2 + 2 * twos:2].set(sink + shifted)
    return sizes[jax.random.permutation(jax.random.fold_in(rng, 2), amount)]


def gaussian(own_key, dims, deviation, bound, split=(), kind=jnp.bfloat16):
    entries = deviation * jax.random.normal(own_key, dims, jnp.float32)
    if split:
        entries = entries * block_scale(own_key, dims, split, -0.22, 0.18)
    return jnp.clip(entries, -bound, bound).astype(kind)


def setup_inputs(seed: int = 0) -> dict:
    splits = jax.random.split(jax.random.key(seed), 8)
    return {
        "layer_input": gaussian(splits[0], (TOKENS, D), (4.0 / TOKENS ** 0.5), 0.09375, ((0, 64), (1, 8))),
        "query_states": draw_query_states(jax.random.fold_in(splits[7], 71), 0),
        "key_states": draw_key_states(jax.random.fold_in(splits[7], 71), 0),
        "value_states": gaussian(splits[3], (TOKENS, KV_HEADS * HEAD_DIM), 1.0, 6.0, ((0, 512),)),
        "out_grad": gaussian(splits[4], (TOKENS, Q_HEADS * HEAD_DIM), 1.0, 6.0, ((0, 512),)),
        "parents": draw_parents(jax.random.fold_in(splits[7], 71), 0),
        "lengths": ragged_sizes(splits[6], TREES, TREES * TREE_LEN * 5 // 8, TREE_LEN, 2).astype(jnp.int32),
    }


def ancestry_of(parent_tree):
    slots = parent_tree.shape[0]
    positions = jnp.arange(slots, dtype=jnp.int32)
    reached = positions[:, None] == positions[None, :]
    jumps = parent_tree.astype(jnp.int32)
    for number in range(max(1, (slots - 1).bit_length())):
        reached = reached | reached[jumps]
        jumps = jumps[jumps]
    return reached


def tree_grads(query_tree, grad_tree, key_tree, value_tree, parent_tree, tree_length):
    scaling = HEAD_DIM ** -0.5
    groups = Q_HEADS // KV_HEADS
    query_heads = query_tree.astype(jnp.float32).reshape(TREE_LEN, KV_HEADS, groups, HEAD_DIM)
    grad_heads = grad_tree.astype(jnp.float32).reshape(TREE_LEN, KV_HEADS, groups, HEAD_DIM)
    key_heads = key_tree.astype(jnp.float32).reshape(TREE_LEN, KV_HEADS, HEAD_DIM)
    value_heads = value_tree.astype(jnp.float32).reshape(TREE_LEN, KV_HEADS, HEAD_DIM)
    positions = jnp.arange(TREE_LEN, dtype=jnp.int32)
    live_pairs = ancestry_of(parent_tree) & (positions < tree_length)[:, None]
    scores = jnp.einsum("ikgd,jkd->kgij", query_heads, key_heads) * scaling
    masked = jnp.where(live_pairs, scores, jnp.float32(-1e30))
    maxima = jnp.max(masked, axis=-1, keepdims=True)
    exponent = jnp.where(live_pairs, jnp.exp(masked - maxima), jnp.float32(0.0))
    row_sums = jnp.sum(exponent, axis=-1, keepdims=True)
    softmax_weights = exponent / jnp.maximum(row_sums, 1.0)
    value_scores = jnp.einsum("ikgd,jkd->kgij", grad_heads, value_heads)
    row_dots = jnp.sum(softmax_weights * value_scores, axis=-1, keepdims=True)
    score_grads = softmax_weights * (value_scores - row_dots) * scaling
    score_round = lax.optimization_barrier(score_grads.astype(jnp.bfloat16)).astype(jnp.float32)
    weight_round = lax.optimization_barrier(softmax_weights.astype(jnp.bfloat16)).astype(jnp.float32)
    key_grad = jnp.einsum("kgij,ikgd->jkd", score_round, query_heads)
    value_grad = jnp.einsum("kgij,ikgd->jkd", weight_round, grad_heads)
    return (key_grad.astype(jnp.bfloat16).reshape(TREE_LEN, KV_HEADS * HEAD_DIM),
            value_grad.astype(jnp.bfloat16).reshape(TREE_LEN, KV_HEADS * HEAD_DIM))


def reference(layer_input, query_states, key_states, value_states, out_grad, parents, lengths):
    trees = lengths.shape[0]
    stacked = (query_states.reshape(trees, TREE_LEN, -1), out_grad.reshape(trees, TREE_LEN, -1),
               key_states.reshape(trees, TREE_LEN, -1), value_states.reshape(trees, TREE_LEN, -1),
               parents.reshape(trees, TREE_LEN), lengths)
    key_grads, value_grads = lax.map(lambda items: tree_grads(*items), stacked)
    key_grads = key_grads.reshape(trees * TREE_LEN, KV_HEADS * HEAD_DIM)
    weight_gradient = jnp.dot(key_grads.T, layer_input, preferred_element_type=jnp.float32)
    return (weight_gradient, value_grads.reshape(trees * TREE_LEN, KV_HEADS * HEAD_DIM))
```

```python
import functools
import jax
import jax.numpy as jnp
from jax import lax
from jax.experimental import pallas as pl
from jax.experimental.pallas import tpu as pltpu
from jax.sharding import Mesh, PartitionSpec as P

HEAD_DIM = 128
TREE_LEN = 512
SCALE = HEAD_DIM ** (-0.5)
LOG2E = 1.4426950408889634
BF16 = jnp.bfloat16
F32 = jnp.float32
NT = (((1,), (1,)), ((), ()))


def pack_kernel(q_ref, g_ref, k_ref, v_ref, out_ref):
    out_ref[0, :, 0:1024] = q_ref[...]
    out_ref[0, :, 1024:2048] = g_ref[...]
    out_ref[0, :, 2048:2304] = k_ref[...]
    out_ref[0, :, 2304:2560] = v_ref[...]


def pack(q, g, k, v):
    return pl.pallas_call(
        pack_kernel,
        grid=(4,),
        in_specs=[
            pl.BlockSpec((128, 1024), lambda i: (0, i)),
            pl.BlockSpec((128, 1024), lambda i: (0, i)),
            pl.BlockSpec((128, 256), lambda i: (0, i)),
            pl.BlockSpec((128, 256), lambda i: (0, i)),
        ],
        out_specs=pl.BlockSpec((1, 128, 2560), lambda i: (i, 0, 0)),
        out_shape=jax.ShapeDtypeStruct((4, 128, 2560), BF16),
        name="pack",
    )(q, g, k, v)


def ancestry_kernel(len_ref, par_ref, bias_ref):
    half = TREE_LEN // 2
    par = par_ref[...]

    def first(j0, i0):
        j = lax.broadcasted_iota(jnp.int32, (half, half), 0) + j0
        i = lax.broadcasted_iota(jnp.int32, (half, half), 1) + i0
        up = par[:, i0:i0 + half]
        return jnp.where((j == i) | (j == up), 1.0, 0.0).astype(BF16)

    def dot(a, b):
        return jnp.dot(a, b, preferred_element_type=F32)

    def flat(x):
        return jnp.where(x > 0.5, 1.0, 0.0).astype(BF16)

    a, b, d = first(0, 0), first(0, half), first(half, half)
    for _ in range(9):
        b = flat(dot(a, b) + dot(b, d))
        a = flat(dot(a, a))
        d = flat(dot(d, d))
    used = lax.broadcasted_iota(jnp.int32, (half, half), 1)
    lo = used < len_ref[0]
    hi = used + half < len_ref[0]
    bias_ref[0:half, 0:half] = jnp.where((a.astype(F32) > 0.5) & lo, 0.0, -1e30)
    bias_ref[0:half, half:] = jnp.where((b.astype(F32) > 0.5) & hi, 0.0, -1e30)
    bias_ref[half:, half:] = jnp.where((d.astype(F32) > 0.5) & hi, 0.0, -1e30)
    bias_ref[half:, 0:half] = jnp.full((half, half), -1e30, F32)


def ancestry(length, parents):
    return pl.pallas_call(
        ancestry_kernel,
        in_specs=[
            pl.BlockSpec(memory_space=pltpu.SMEM),
            pl.BlockSpec(memory_space=pltpu.VMEM),
        ],
        out_specs=pl.BlockSpec(memory_space=pltpu.VMEM),
        out_shape=jax.ShapeDtypeStruct((TREE_LEN, TREE_LEN), F32),
        cost_estimate=pl.CostEstimate(
            flops=9 * 8 * 256**3, bytes_accessed=1 << 20, transcendentals=0
        ),
        name="ancestry",
    )(length, parents)


def attention_kernel(pk_ref, bias_ref, kt_ref, dv_ref, dk_acc, dv_acc):
    for kv in range(2):
        dk_acc[...] = jnp.zeros_like(dk_acc)
        dv_acc[...] = jnp.zeros_like(dv_acc)
        k0 = 2048 + kv * 128
        v0 = 2304 + kv * 128
        for ib in range(4):
            rows = slice(ib * 128, (ib + 1) * 128)
            jr = (ib + 1) * 128
            heads = [(kv * 4 + g) * 128 for g in range(4)]
            q = jnp.concatenate([pk_ref[rows, h:h + 128] for h in heads], axis=0)
            do = jnp.concatenate(
                [pk_ref[rows, 1024 + h:1024 + h + 128] for h in heads], axis=0
            )
            s = lax.dot_general(
                pk_ref[0:jr, k0:k0 + 128], q, NT, preferred_element_type=F32
            )
            b = bias_ref[0:jr, rows]
            t = s * (SCALE * LOG2E) + jnp.concatenate([b] * 4, axis=1)
            m = jnp.maximum(jnp.max(t, axis=0, keepdims=True), -1e29)
            e = jnp.exp2(t - m)
            r = 1.0 / jnp.maximum(jnp.sum(e, axis=0, keepdims=True), 1.0)
            w = e * r
            vs = lax.dot_general(
                pk_ref[0:jr, v0:v0 + 128], do, NT, preferred_element_type=F32
            )
            rd = jnp.sum(w * vs, axis=0, keepdims=True)
            ds = (w * (vs - rd) * SCALE).astype(BF16)
            dk_acc[0:jr, :] += jnp.dot(ds, q, preferred_element_type=F32)
            dv_acc[0:jr, :] += jnp.dot(w.astype(BF16), do, preferred_element_type=F32)
        dk_t = dk_acc[...].T.astype(BF16)
        for part in range(2):
            for owner in range(4):
                lo = part * 64 + owner * 16
                piece = dk_t[lo:lo + 16, :]
                to = (kv * 2 + part) * 16
                for copy in range(8):
                    kt_ref[owner * 8 + copy, to:to + 16, :] = piece
        for jb in range(4):
            dv_ref[jb, :, kv * 128:(kv + 1) * 128] = dv_acc[
                jb * 128:(jb + 1) * 128, :
            ].astype(BF16)


def attention(packed, bias):
    return pl.pallas_call(
        attention_kernel,
        in_specs=[pl.BlockSpec(memory_space=pltpu.VMEM)] * 2,
        out_specs=[pl.BlockSpec(memory_space=pltpu.VMEM)] * 2,
        out_shape=[
            jax.ShapeDtypeStruct((32, 64, TREE_LEN), BF16),
            jax.ShapeDtypeStruct((4, 128, 256), BF16),
        ],
        scratch_shapes=[pltpu.VMEM((TREE_LEN, 128), F32)] * 2,
        cost_estimate=pl.CostEstimate(
            flops=8 * 8 * 512 * 512 * 128, bytes_accessed=6 << 20, transcendentals=1 << 21
        ),
        name="attention",
    )(packed, bias)


def weight_kernel(own_ref, a_ref, l0, l1, l2, l3, out_ref, acc):
    r, t = pl.program_id(0), pl.program_id(1)

    @pl.when((r == 0) & (t == 0))
    def _():
        acc[...] = jnp.zeros_like(acc)

    for at, ref in enumerate((l0, l1, l2, l3)):
        @pl.when(r == at)
        def _(ref=ref):
            acc[...] += jnp.dot(a_ref[0], ref[0], preferred_element_type=F32)

    @pl.when((r == 3) & (t == 1))
    def _():
        out_ref[...] = acc[...].astype(BF16)


def weight(own, a, layers):
    def layer_map(at):
        def index(r, t, own_ref):
            return (jnp.where(r == at, t, jnp.where(r < at, 0, 1)), 0, 0)

        return index

    def a_map(r, t, own_ref):
        return ((own_ref[0] ^ r) * 2 + t, 0, 0)

    return pl.pallas_call(
        weight_kernel,
        grid_spec=pltpu.PrefetchScalarGridSpec(
            num_scalar_prefetch=1,
            grid=(4, 2),
            in_specs=[pl.BlockSpec((1, 256, 512), a_map)]
            + [pl.BlockSpec((1, 512, 1024), layer_map(at)) for at in range(4)],
            out_specs=pl.BlockSpec((256, 1024), lambda r, t, own_ref: (0, 0)),
            scratch_shapes=[pltpu.VMEM((256, 1024), F32)],
        ),
        out_shape=jax.ShapeDtypeStruct((256, 1024), BF16),
        cost_estimate=pl.CostEstimate(
            flops=2 * 256 * 4096 * 1024, bytes_accessed=11 << 20, transcendentals=0
        ),
        name="weight",
    )(own, a, *layers)


def local(layer_input, query_states, key_states, value_states, out_grad, parents, lengths):
    tree = lax.axis_index("xh")
    own = lax.axis_index("xl") * 2 + lax.axis_index("c")
    swap = [(0, 1), (1, 0)]

    packed = pack(query_states, out_grad, key_states, value_states)
    packed = lax.all_to_all(packed, "y", 0, 0, tiled=True).reshape(TREE_LEN, 2560)

    far = lax.ppermute(layer_input, "xl", swap)
    mate = lax.ppermute(layer_input, "c", swap)
    far_mate = lax.ppermute(far, "c", swap)

    parent_tree = lax.dynamic_slice_in_dim(parents.reshape(2, TREE_LEN), tree, 1, axis=0)
    length = lax.dynamic_slice_in_dim(lengths, tree, 1, axis=0)
    bias = ancestry(length, parent_tree)

    key_parts, value_parts = attention(packed, bias)
    gathered = lax.all_to_all(key_parts, ("xl", "c", "xh", "y"), 0, 0, tiled=True)
    value_grads = lax.all_to_all(value_parts, "y", 0, 0, tiled=True)

    layers = [x.reshape(2, TREE_LEN, 1024) for x in (layer_input, mate, far, far_mate)]
    partial = weight(own.astype(jnp.int32).reshape(1), gathered.reshape(8, 256, TREE_LEN), layers)
    shares = lax.all_to_all(partial.reshape(16, 16, 1024), "z", 0, 0, tiled=True)
    weight_gradient = jnp.sum(shares.astype(F32), axis=0)
    value_gradient = value_grads.transpose(1, 0, 2).reshape(128, 1024)
    return (weight_gradient, value_gradient)


def solution(mesh):
    fine = Mesh(mesh.devices.reshape(16, 2, 2, 2, 4), ("z", "xl", "c", "xh", "y"))
    dp, head = ("z", "xl", "c"), ("xh", "y")
    rows = P(dp + head, None)
    return jax.shard_map(
        local,
        mesh=fine,
        in_specs=(P(dp, head), rows, rows, rows, rows, P(dp), P(dp)),
        out_specs=(P(dp, head), rows),
        check_vma=False,
    )
```
